512 devices in a mesh: dp: 16 (over y, core), table: 32 (over x, z).
Axes of the slice: x: 4, y: 8, z: 8, core: 2. Of those that a mesh axis runs over, the one named last changes fastest.
Arguments:
- embedded: bfloat16 [2, 32768, 4096], P(None, 'dp', 'table'), may hold values from -1.1953125 to 1.1953125
- resid_grad: bfloat16 [2, 32768, 4096], P(None, 'dp', 'table'), may hold values from -0.29882812 to 0.29882812
- query_grad: bfloat16 [2, 32768, 2048], P(None, ('dp', 'table')), may hold values from -0.59765625 to 0.59765625
- query_weight: bfloat16 [4096, 2048], P('table'), may hold values from -0.09375 to 0.09375
- ngram_rows: int32 [2, 32768, 4], P(None, 'dp'), may hold values from 0 to 3199999, as said below
- touched_rows: int32 [32, 4, 12], replicated, may hold values from -1 to 3199999, as said below
- row_values: float32 [32, 4, 12, 1024], P('table'), may hold values from -6 to 6
- row_mean: float32 [32, 4, 12, 1024], P('table'), may hold values from -0.6 to 0.6
- row_square: float32 [32, 4, 12, 1024], P('table'), may hold values from 0.01 to 0.1
Outputs:
- weight_grad: float32 [4096, 2048], P('table')
- new_values: float32 [32, 4, 12, 1024], P('table')
- new_mean: float32 [32, 4, 12, 1024], P('table')
- new_square: float32 [32, 4, 12, 1024], P('table')
The draws below stay inside these ranges and needn't reach their ends.
Inputs may be any that keep to these rules, and one draw needn't show every extreme that they name: `touched_rows`: owner o's list for slice s holds 1 to 12 distinct row ids of [o * 100000, (o + 1) * 100000) first, then -1; in every slice some owner's list is full. `ngram_rows`: every id of slice s is one of the listed rows of owner id // 100000 for slice s.
All inputs are finite; a program needn't handle non-finite values.
Results may differ from the reference program's by a relative error of at most 0.0003.
Values may be sent and summed in bfloat16 or wider, within the bound.
No kernel may reach another device: no remote copies, remote signals or barrier semaphores. Data moves between devices by JAX's collectives and lax.ppermute only.
A program may use at most 64 MiB of HBM per device.

```python
import math
import jax
import jax.numpy as jnp

SLICES = 4
SW = 1024
D = 4096
HQ = 2048
MICRO = 2
US = 12
SHARD_ROWS = 100000
TOKENS = 32768
N_TABLE = 32


def listed_rows(key):
    base = jax.random.fold_in(key, 7)
    key_count, key_full, key_offset = jax.random.split(base, 3)
    counts = jax.random.randint(key_count, (N_TABLE, SLICES), 1, US + 1)
    fullest = jax.random.randint(key_full, (SLICES,), 0, N_TABLE)
    owners = jnp.arange(N_TABLE, dtype=jnp.int32)
    counts = jnp.where(owners[:, None] == fullest[None, :], US, counts).astype(jnp.int32)
    stride = SHARD_ROWS // US
    offsets = jax.random.randint(key_offset, (N_TABLE, SLICES, US), 0, stride)
    entries = jnp.arange(US, dtype=jnp.int32)
    rows = owners[:, None, None] * SHARD_ROWS + entries[None, None, :] * stride + offsets
    live = entries[None, None, :] < counts[:, :, None]
    return (jnp.where(live, rows, -1).astype(jnp.int32), counts)


def draw_touched_rows(key, part):
    return listed_rows(key)[0]


def draw_ngram_rows(key, part):
    lists, counts = listed_rows(key)
    starts = jnp.cumsum(counts, axis=0) - counts
    totals = jnp.sum(counts, axis=0)
    picks = jax.random.randint(jax.random.fold_in(key, 11), (MICRO, TOKENS, SLICES), 0, totals[None, None, :])
    starts_t = starts.T
    owner = jnp.sum((picks[..., None] >= starts_t[None, None, :, :]).astype(jnp.int32), axis=-1) - 1
    chosen = jnp.arange(N_TABLE, dtype=jnp.int32)[None, None, None, :] == owner[..., None]
    first = jnp.sum(jnp.where(chosen, starts_t[None, None, :, :], 0), axis=-1)
    entry = picks - first
    slot_ids = jnp.arange(SLICES, dtype=jnp.int32)[None, None, :]
    return lists[owner, slot_ids, entry].astype(jnp.int32)


def shard_levels(rng, dims, cuts, least, top_value):
    factor_of, own = 1.0, jax.random.fold_in(rng, 6)
    for dim, blocks in cuts:
        heights = jnp.exp(jax.random.uniform(jax.random.fold_in(own, dim), (blocks,), jnp.float32, least / len(cuts), top_value / len(cuts)))
        factor_of = factor_of * jnp.repeat(heights, dims[dim] // blocks).reshape([-1 if axis == dim else 1 for axis in range(len(dims))])
    return factor_of


def bell_draw(key, shape, spread, limit, shards=(), held_as=jnp.bfloat16):
    factor_of = shard_levels(key, shape, shards, -0.22, 0.18) if shards else 1.0
    drawn = jax.random.normal(key, shape, jnp.float32) * spread * factor_of
    return jnp.minimum(jnp.maximum(drawn, -limit), limit).astype(held_as)


def setup_inputs(seed: int = 0) -> dict:
    splits = jax.random.split(jax.random.key(seed), 10)
    return {
        "embedded": bell_draw(splits[0], (MICRO, TOKENS, D), 0.2, 1.1953125, ((1, 16), (2, 32))),
        "resid_grad": bell_draw(splits[1], (MICRO, TOKENS, D), 0.05, 0.29882812, ((1, 16), (2, 32))),
        "query_grad": bell_draw(splits[2], (MICRO, TOKENS, HQ), 0.1, 0.59765625, ((1, 512),)),
        "query_weight": bell_draw(splits[3], (D, HQ), D ** -0.5, 0.09375, ((0, 32),)),
        "ngram_rows": draw_ngram_rows(jax.random.fold_in(splits[9], 71), 0),
        "touched_rows": draw_touched_rows(jax.random.fold_in(splits[9], 71), 0),
        "row_values": bell_draw(splits[6], (N_TABLE, SLICES, US, SW), 1.0, 6.0, ((0, 32),), jnp.float32),
        "row_mean": bell_draw(splits[7], (N_TABLE, SLICES, US, SW), 0.1, 0.6, ((0, 32),), jnp.float32),
        "row_square": jnp.clip(jnp.exp(math.log(0.1) - 2.3025851 * jax.random.uniform(splits[8], (N_TABLE, SLICES, US, SW), jnp.float32) ** shard_levels(splits[8], (N_TABLE, SLICES, US, SW), ((0, 32),), -0.2, 0.2)), 0.01, 0.1),
    }


beta_one = 0.9
beta_two = 0.95
learn_rate = 0.01
adam_eps = 1e-08
adam_step = 10

def adam_rows(grads, values, mean, square, live):
    corr_one = 1.0 - beta_one ** adam_step
    corr_two = 1.0 - beta_two ** adam_step
    mean_next = beta_one * mean + (1.0 - beta_one) * grads
    square_next = beta_two * square + (1.0 - beta_two) * grads * grads
    update = learn_rate * (mean_next / corr_one) / (jnp.sqrt(square_next / corr_two) + adam_eps)
    values_next = values - update
    return (jnp.where(live, values_next, values), jnp.where(live, mean_next, mean), jnp.where(live, square_next, square))

def reference(embedded, resid_grad, query_grad, query_weight, ngram_rows, touched_rows, row_values, row_mean, row_square):
    wgrad = jnp.zeros((D, HQ), jnp.float32)
    seg_total = jnp.zeros((SLICES, N_TABLE * US, SW), jnp.float32)
    for micro in range(MICRO):
        back = jnp.dot(query_grad[micro], query_weight.T, preferred_element_type=jnp.float32)
        emb_grad = resid_grad[micro].astype(jnp.float32) + back
        wgrad = wgrad + jnp.dot(embedded[micro].T, query_grad[micro], preferred_element_type=jnp.float32)
        for slot in range(SLICES):
            ids = ngram_rows[micro, :, slot]
            owner = (ids // SHARD_ROWS).astype(jnp.int32)
            listed = touched_rows[owner, slot, :]
            where_hit = jnp.argmax((listed == ids[:, None]).astype(jnp.int32), axis=1).astype(jnp.int32)
            segment = owner * US + where_hit
            piece = emb_grad[:, slot * SW:(slot + 1) * SW]
            summed = jax.ops.segment_sum(piece, segment, num_segments=N_TABLE * US)
            seg_total = seg_total.at[slot].add(summed)
    grads = seg_total.reshape(SLICES, N_TABLE, US, SW).transpose(1, 0, 2, 3)
    live = (touched_rows >= 0)[..., None]
    values_next, mean_next, square_next = adam_rows(grads, row_values, row_mean, row_square, live)
    return (wgrad, values_next, mean_next, square_next)
```

```python
import jax
import jax.numpy as jnp
from jax import lax
from jax.sharding import Mesh, PartitionSpec as P

SW = 1024

beta_one = 0.9
beta_two = 0.95
learn_rate = 0.01
adam_eps = 1e-08
adam_step = 10

f32 = jnp.float32
bf16 = jnp.bfloat16


def adam_rows(grads, values, mean, square, live):
    corr_one = 1.0 - beta_one**adam_step
    corr_two = 1.0 - beta_two**adam_step
    mean_next = beta_one * mean + (1.0 - beta_one) * grads
    square_next = beta_two * square + (1.0 - beta_two) * grads * grads
    update = learn_rate * (mean_next / corr_one) / (jnp.sqrt(square_next / corr_two) + adam_eps)
    values_next = values - update
    return (
        jnp.where(live, values_next, values),
        jnp.where(live, mean_next, mean),
        jnp.where(live, square_next, square),
    )


def over_tokens(left, right):
    return lax.dot_general(left, right, (((0,), (0,)), ((), ())), preferred_element_type=f32)


def shift(array, axis, step):
    size = lax.axis_size(axis)
    return lax.ppermute(array, axis, [(i, (i + step) % size) for i in range(size)])


def local(
    embedded,
    resid_grad,
    query_grad,
    query_weight,
    ngram_rows,
    touched_rows,
    row_values,
    row_mean,
    row_square,
):
    micro, group, width = embedded.shape
    per, hidden = query_grad.shape[1:]
    nx, nz, ny = lax.axis_size("x"), lax.axis_size("z"), lax.axis_size("y")
    x_idx, z_idx, core = lax.axis_index("x"), lax.axis_index("z"), lax.axis_index("core")
    tables, slices, entries = touched_rows.shape
    part = hidden // nx
    tokens = micro * group
    groups = ny * 2
    rows_p = width // groups

    def token_order(array):
        tail = array.shape[2:]
        array = array.reshape((micro, nx, nz, per) + tail)
        return array.transpose((2, 1, 0, 3) + tuple(range(4, array.ndim))).reshape((tokens,) + tail)

    def by_part(array):
        return array.reshape(-1, nx, part).transpose(1, 0, 2)

    query = lax.all_to_all(by_part(query_grad), "x", 0, 0, tiled=True)
    query = lax.all_gather(query.reshape(nx * micro * per, part), "z", axis=0, tiled=True)

    weight = lax.all_to_all(by_part(query_weight), "x", 0, 0, tiled=True)

    emb = token_order(embedded)
    half = tokens // 2
    emb_back = shift(emb, "x", 1)
    emb_front = shift(emb, "x", -1)
    far_low = shift(emb_back[:half], "x", 1)
    far_high = shift(emb_front[half:], "x", -1)
    emb_far = jnp.concatenate([far_low, far_high], axis=0)
    emb_all = [emb, emb_front, emb_far, emb_back]

    ids = token_order(ngram_rows)
    lists = touched_rows.transpose(1, 2, 0).reshape(slices, entries * tables)

    def onehot(ids_of, list_of):
        return (ids_of[:, None] == list_of[None, :]).astype(bf16)

    own_ids = lax.dynamic_index_in_dim(ids, x_idx, 1, False)
    own_list = lax.dynamic_index_in_dim(lists, x_idx, 0, False)
    resid_rows = over_tokens(onehot(own_ids, own_list), token_order(resid_grad))

    row_parts = []
    for s in range(slices):
        seg = over_tokens(onehot(ids[:, s], lists[s]), query)
        high = lax.reduce_precision(seg, 8, 7)
        low = (seg - high).astype(bf16)
        one = lax.dot_general(high.astype(bf16), weight[s], (((1,), (1,)), ((), ())), preferred_element_type=f32)
        two = lax.dot_general(low, weight[s], (((1,), (1,)), ((), ())), preferred_element_type=f32)
        row_parts.append(one + two + jnp.where(x_idx == s, resid_rows, 0.0))
    row_sum = jnp.stack(row_parts).reshape(groups, slices * entries // groups * tables, width)

    w_parts = [over_tokens(piece, query) for piece in emb_all]
    w_sum = jnp.stack(w_parts)
    lanes = 128
    w_sum = w_sum.reshape(nx, groups, rows_p, part // lanes, lanes).transpose(1, 0, 3, 2, 4)
    w_sum = w_sum.reshape(groups, nx * part // lanes * rows_p, lanes)
    both = jnp.concatenate([w_sum, row_sum], axis=1)
    both = both.reshape(ny, 2, both.shape[1], lanes)
    first = core == 0
    send = jnp.where(first, both[:, 1], both[:, 0])
    keep = jnp.where(first, both[:, 0], both[:, 1])
    pair = keep + shift(send, "core", 1)
    pieces = lax.all_to_all(pair, "y", 0, 0, tiled=True)
    total = jnp.sum(pieces, axis=0)

    w_rows = nx * part // lanes * rows_p
    w_mine = total[:w_rows].reshape(nx, part // lanes * rows_p, lanes)
    twice = jnp.concatenate([w_mine, w_mine], axis=0)
    w_mine = lax.dynamic_slice_in_dim(twice, nx - x_idx, nx, 0)
    w_mine = lax.all_to_all(w_mine, "x", 0, 0, tiled=True).reshape(w_rows, lanes)

    pairs = slices * entries // groups
    r_mine = total[w_rows:].reshape(pairs, tables, width).transpose(1, 0, 2)
    r_mine = lax.all_to_all(r_mine, ("x", "z"), 0, 0, tiled=True)
    r_mine = jnp.sum(r_mine.reshape(nx, nz, pairs, width), axis=0)
    r_mine = r_mine.transpose(1, 0, 2).reshape(pairs * nz, lanes)

    piece = jnp.concatenate([w_mine, r_mine], axis=0)
    spread = jnp.broadcast_to(piece[None], (ny,) + piece.shape)
    mine = lax.all_to_all(spread, "y", 0, 0, tiled=True)
    other = shift(mine, "core", 1)
    full = jnp.stack([jnp.where(first, mine, other), jnp.where(first, other, mine)], axis=1)
    full = full.reshape((groups,) + piece.shape)
    weight_grad = full[:, :w_rows].reshape(groups, hidden // lanes, rows_p, lanes)
    weight_grad = weight_grad.transpose(0, 2, 1, 3).reshape(width, hidden)
    grads = full[:, w_rows:].reshape(slices, entries, nz * width)

    mine_rows = lax.dynamic_index_in_dim(touched_rows, x_idx * nz + z_idx, 0, False)
    live = (mine_rows >= 0)[..., None]
    values_next, mean_next, square_next = adam_rows(grads, row_values[0], row_mean[0], row_square[0], live)
    return (weight_grad, values_next[None], mean_next[None], square_next[None])


def solution(mesh):
    fine = Mesh(mesh.devices.reshape(8, 2, 4, 8), ("y", "core", "x", "z"))
    dp, table = ("y", "core"), ("x", "z")
    placed = (
        P(None, dp, table),
        P(None, dp, table),
        P(None, dp + table, None),
        P(table, None),
        P(None, dp, None),
        P(),
        P(table, None, None, None),
        P(table, None, None, None),
        P(table, None, None, None),
    )
    return jax.shard_map(
        local,
        mesh=fine,
        in_specs=placed,
        out_specs=(
            P(table, None),
            P(table, None, None, None),
            P(table, None, None, None),
            P(table, None, None, None),
        ),
        check_vma=False,
    )
```

```python
import jax
import jax.numpy as jnp
from jax import lax
from jax.experimental import pallas as pl
from jax.experimental.pallas import tpu as pltpu
from jax.sharding import Mesh, PartitionSpec as P


LANES = 128

beta_one = 0.9
beta_two = 0.95
learn_rate = 0.01
adam_eps = 1e-08
adam_step = 10

f32 = jnp.float32
bf16 = jnp.bfloat16


def adam_rows(grads, values, mean, square, live):
    corr_one = 1.0 - beta_one**adam_step
    corr_two = 1.0 - beta_two**adam_step
    mean_next = beta_one * mean + (1.0 - beta_one) * grads
    square_next = beta_two * square + (1.0 - beta_two) * grads * grads
    update = learn_rate * (mean_next / corr_one) / (jnp.sqrt(square_next / corr_two) + adam_eps)
    values_next = values - update
    return (
        jnp.where(live, values_next, values),
        jnp.where(live, mean_next, mean),
        jnp.where(live, square_next, square),
    )


def over_tokens(left, right):
    return lax.dot_general(left, right, (((0,), (0,)), ((), ())), preferred_element_type=f32)


def shift(array, axis, step):
    size = lax.axis_size(axis)
    return lax.ppermute(array, axis, [(i, (i + step) % size) for i in range(size)])


def blocks_kernel(counts, first, last, slices, zs, *refs):
    refs = list(refs)
    queries = [refs.pop(0) for _ in counts]
    chunks = len(zs)
    embs = [[refs.pop(0) for _ in range(4)] for _ in range(chunks)]
    ids = [refs.pop(0) for _ in range(chunks)]
    lists = refs.pop(0)
    acc = None if first else refs.pop(0)
    if last:
        weight, resid, place = refs.pop(0), refs.pop(0), refs.pop(0)
    out, left, right = refs
    per = left.shape[1] // chunks
    width = embs[0][0].shape[1]
    start = 0
    for ref, count in zip(queries, counts):
        right[start : start + count, :] = ref[...]
        start += count
    k_rows = lists.shape[0]
    for c in range(chunks):
        cols = slice(c * per, (c + 1) * per)
        for o in range(4):
            left[o * width : (o + 1) * width, cols] = embs[c][o][0]
        for s in range(slices):
            hit = lists[:, s : s + 1] == ids[c][0, s : s + 1, :]
            rows = slice(4 * width + s * k_rows, 4 * width + (s + 1) * k_rows)
            left[rows, cols] = jnp.where(hit, 1.0, 0.0).astype(bf16)
    total = jnp.dot(left[: 4 * width, :], right[...], preferred_element_type=f32)
    if not first:
        total = total + acc[: 4 * width, :]
    if last:
        groups = out.shape[0]
        tiles = total.shape[1] // LANES
        height = width // groups
        for o in range(4):
            for t in range(tiles):
                at = (o * tiles + t) * height
                block = total[o * width : (o + 1) * width, t * LANES : (t + 1) * LANES]
                out[:, at : at + height, :] = block.reshape(groups, height, LANES)
    else:
        out[: 4 * width, :] = total
    for s in range(slices):
        rows = slice(4 * width + s * k_rows, 4 * width + (s + 1) * k_rows)
        total = jnp.dot(left[rows, :], right[...], preferred_element_type=f32)
        if not first:
            total = total + acc[rows, :]
        if not last:
            out[rows, :] = total
            continue
        high = total.astype(bf16)
        low = (total - high.astype(f32)).astype(bf16)
        turned = (((1,), (1,)), ((), ()))
        grads = lax.dot_general(high, weight[s], turned, preferred_element_type=f32)
        grads = grads + lax.dot_general(low, weight[s], turned, preferred_element_type=f32)
        grads = grads + jnp.where(place[0] == s, resid[...], 0.0)
        share = groups // slices
        out[s * share : (s + 1) * share, 4 * tiles * height :, :] = grads.reshape(share, k_rows // share, width)


def add_blocks(queries, zs, embs, ids, lists, acc=None, tail=None):
    chunks = len(zs)
    width, per = embs[0].shape[1:]
    part = queries[0].shape[1]
    slices = ids.shape[1]
    k_rows = lists.shape[0]
    rows = 4 * width + slices * k_rows
    counts = tuple(q.shape[0] for q in queries)

    def whole(array):
        return pl.BlockSpec(array.shape, lambda i, z: (0,) * array.ndim)

    def at(array, c):
        return pl.BlockSpec((1,) + array.shape[1:], lambda i, z: (z[c],) + (0,) * (array.ndim - 1))

    operands, specs = list(queries), [whole(q) for q in queries]
    for c in range(chunks):
        for emb in embs:
            operands.append(emb)
            specs.append(at(emb, c))
    for c in range(chunks):
        operands.append(ids)
        specs.append(at(ids, c))
    operands.append(lists)
    specs.append(whole(lists))
    if acc is not None:
        operands.append(acc)
        specs.append(whole(acc))
    if tail is None:
        out = jax.ShapeDtypeStruct((rows, part), f32)
    else:
        weight, resid, place, groups = tail
        operands += [weight, resid, place]
        specs += [whole(weight), whole(resid), pl.BlockSpec(memory_space=pltpu.SMEM)]
        out = jax.ShapeDtypeStruct((groups, 4 * width * part // groups // LANES + slices * k_rows // groups, LANES), f32)

    def kernel(z_ref, *refs):
        blocks_kernel(counts, acc is None, tail is not None, slices, zs, *refs)

    tokens = chunks * per
    return pl.pallas_call(
        kernel,
        grid_spec=pltpu.PrefetchScalarGridSpec(
            num_scalar_prefetch=1,
            grid=(1,),
            in_specs=specs,
            out_specs=whole(out),
            scratch_shapes=[pltpu.VMEM((rows, tokens), bf16), pltpu.VMEM((tokens, part), bf16)],
        ),
        out_shape=out,
        cost_estimate=pl.CostEstimate(
            flops=2 * rows * tokens * part, transcendentals=0, bytes_accessed=4 * rows * part + 2 * tokens * part
        ),
    )(jnp.stack(zs).astype(jnp.int32), *operands)


def local(
    embedded,
    resid_grad,
    query_grad,
    query_weight,
    ngram_rows,
    touched_rows,
    row_values,
    row_mean,
    row_square,
):
    micro, group, width = embedded.shape
    per, hidden = query_grad.shape[1:]
    nx, nz, ny = lax.axis_size("x"), lax.axis_size("z"), lax.axis_size("y")
    x_idx, z_idx, core = lax.axis_index("x"), lax.axis_index("z"), lax.axis_index("core")
    tables, slices, entries = touched_rows.shape
    part = hidden // nx
    groups = ny * 2
    rows_p = width // groups
    chunk = nx * micro * per
    lanes = LANES

    def by_z(array):
        array = array.reshape(micro, nx, nz, per, array.shape[2])
        return array.transpose(2, 4, 1, 0, 3).reshape(nz, -1, chunk)

    def by_part(array):
        return array.reshape(-1, nx, part).transpose(1, 0, 2)

    query = lax.all_to_all(by_part(query_grad), "x", 0, 0, tiled=True).reshape(chunk, part)
    lower, upper = [query], [query]
    for _ in range(nz // 2 - 1):
        lower.append(shift(lower[-1], "z", 1))
        upper.append(shift(upper[-1], "z", -1))
    far_query = [shift(lower[-1][: chunk // 2], "z", 1), shift(upper[-1][chunk // 2 :], "z", -1)]

    emb = by_z(embedded)
    half = nz // 2
    emb_back = shift(emb, "x", 1)
    emb_front = shift(emb, "x", -1)
    far_low = shift(emb_back[:half], "x", 1)
    far_high = shift(emb_front[half:], "x", -1)
    emb_far = jnp.concatenate([far_low, far_high], axis=0)
    embs = [emb, emb_front, emb_far, emb_back]

    weight = lax.all_to_all(by_part(query_weight), "x", 0, 0, tiled=True)

    ids = by_z(ngram_rows)
    lists = touched_rows.transpose(2, 0, 1).reshape(entries * tables, slices)

    own_ids = lax.dynamic_index_in_dim(ngram_rows, x_idx, 2, False).reshape(micro * group)
    own_list = lax.dynamic_index_in_dim(touched_rows, x_idx, 1, False).T.reshape(entries * tables)
    onehot = (own_ids[:, None] == own_list[None, :]).astype(bf16)
    resid_rows = over_tokens(onehot, resid_grad.reshape(micro * group, width))

    def place(step):
        return lax.rem(z_idx + step + nz, nz)

    acc = add_blocks(
        [query, lower[1], upper[1], lower[2], upper[2]],
        [place(0), place(-1), place(1), place(-2), place(2)],
        embs, ids, lists,
    )
    acc = add_blocks([lower[3], upper[3]], [place(-3), place(3)], embs, ids, lists, acc)
    both = add_blocks(
        far_query, [place(4)], embs, ids, lists, acc,
        (weight, resid_rows, x_idx.astype(jnp.int32)[None], groups),
    )
    both = both.reshape(ny, 2, both.shape[1], lanes)
    first = core == 0
    send = jnp.where(first, both[:, 1], both[:, 0])
    keep = jnp.where(first, both[:, 0], both[:, 1])
    pair = keep + shift(send, "core", 1)
    pieces = lax.all_to_all(pair, "y", 0, 0, tiled=True)
    total = jnp.sum(pieces, axis=0)

    w_rows = nx * part // lanes * rows_p
    w_mine = total[:w_rows].reshape(nx, part // lanes * rows_p, lanes)
    w_mine = [w_mine[0]] + [shift(w_mine[o], "x", o) for o in range(nx - 1, 0, -1)]
    w_mine = jnp.stack(w_mine + w_mine)
    w_mine = lax.dynamic_slice_in_dim(w_mine, nx - x_idx, nx, 0).reshape(w_rows, lanes)

    pairs = slices * entries // groups
    r_mine = total[w_rows:].reshape(pairs, tables, width).transpose(1, 0, 2)
    r_mine = lax.all_to_all(r_mine, ("x", "z"), 0, 0, tiled=True)
    r_mine = jnp.sum(r_mine.reshape(nx, nz, pairs, width), axis=0)
    r_mine = r_mine.transpose(1, 0, 2).reshape(pairs * nz, lanes)

    piece = jnp.concatenate([w_mine, r_mine], axis=0)
    spread = jnp.broadcast_to(piece[None], (ny,) + piece.shape)
    mine = lax.all_to_all(spread, "y", 0, 0, tiled=True)
    other = shift(mine, "core", 1)
    full = jnp.stack([jnp.where(first, mine, other), jnp.where(first, other, mine)], axis=1)
    full = full.reshape((groups,) + piece.shape)
    weight_grad = full[:, :w_rows].reshape(groups, hidden // lanes, rows_p, lanes)
    weight_grad = weight_grad.transpose(0, 2, 1, 3).reshape(width, hidden)
    grads = full[:, w_rows:].reshape(slices, entries, nz * width)

    mine_rows = lax.dynamic_index_in_dim(touched_rows, x_idx * nz + z_idx, 0, False)
    live = (mine_rows >= 0)[..., None]
    values_next, mean_next, square_next = adam_rows(grads, row_values[0], row_mean[0], row_square[0], live)
    return (weight_grad, values_next[None], mean_next[None], square_next[None])


def solution(mesh):
    fine = Mesh(mesh.devices.reshape(8, 2, 4, 8), ("y", "core", "x", "z"))
    dp, table = ("y", "core"), ("x", "z")
    placed = (
        P(None, dp, table),
        P(None, dp, table),
        P(None, dp + table, None),
        P(table, None),
        P(None, dp, None),
        P(),
        P(table, None, None, None),
        P(table, None, None, None),
        P(table, None, None, None),
    )
    return jax.shard_map(
        local,
        mesh=fine,
        in_specs=placed,
        out_specs=(
            P(table, None),
            P(table, None, None, None),
            P(table, None, None, None),
            P(table, None, None, None),
        ),
        check_vma=False,
    )
```
